512 devices in a mesh: rows: 128 (over y_lo, x, z, core), rep: 4 (over y_hi).
Axes of the slice: x: 4, y: 8 (y_hi: 4, y_lo: 2; y = y_hi * 2 + y_lo), z: 8, core: 2. Of those that a mesh axis runs over, the one named last changes fastest.
Arguments:
- node_feats: bfloat16 [131072, 256], P('rows'), may hold values from -6 to 6
- weight: bfloat16 [256, 256], replicated, may hold values from -0.375 to 0.375
- cotangent: bfloat16 [131072, 256], P('rows'), may hold values from -6 to 6
- tile_values: bfloat16 [128, 5, 32, 128, 128], P('rows', None, 'rep'), may hold values from -1 to 1, as said below
- tile_coords: int32 [2, 128, 5, 32], P(None, 'rows', None, 'rep'), may hold values from 0 to 7, as said below
- tile_counts: int32 [128, 5], P('rows'), may hold values from 0 to 32, as said below
Outputs:
- activated: bfloat16 [131072, 256], P('rows')
- input_grad: bfloat16 [131072, 256], P('rows')
- weight_grad: float32 [256, 256], replicated
The draws below stay inside these ranges and needn't reach their ends.
Inputs may be any that keep to these rules, and one draw needn't show every extreme that they name: tile_counts[r, d] = tile_counts[(r + d - 2) mod 128, 4 - d]; tile_counts[r, 2] = 32. tile_coords[0, r, d, k] = tile_coords[1, s, 4 - d, k] and tile_coords[1, r, d, k] = tile_coords[0, s, 4 - d, k] with s = (r + d - 2) mod 128, for d other than 2; for d = 2, slots 2m and 2m + 1 hold swapped coordinates. tile_values[r, d, k] is the transpose of tile_values[s, 4 - d, k] with s as above for d other than 2; for d = 2, slot 2m + 1 is the transpose of slot 2m.
All inputs are finite; a program needn't handle non-finite values.
Results may differ from the reference program's by a relative error of at most 0.006.
Values may be sent and summed in bfloat16 or wider, within the bound.
A program may use at most 64 MiB of HBM per device.

```python
import jax
import jax.numpy as jnp
from jax import lax

F = 256
TILE = 128
BLK = 8
HOPS = 2
SLOT_DEV = 8
REACH = 5
SLOTS = 32
GROUPS = 128
NODES = 131072


def partner_index():
    index = jnp.arange(GROUPS, dtype=jnp.int32)
    offsets = jnp.arange(REACH, dtype=jnp.int32)
    joined = (index[:, None] + offsets[None, :] - HOPS) % GROUPS
    mirror = jnp.broadcast_to(2 * HOPS - offsets[None, :], (GROUPS, REACH))
    return (joined, mirror, offsets)


def pair_layout(key):
    combos = BLK * BLK
    joined, mirror, offsets = partner_index()
    hub = jax.random.randint(jax.random.fold_in(key, 11), (GROUPS,), 0, 3).astype(jnp.int32)
    pick = jax.random.randint(jax.random.fold_in(key, 12), (GROUPS, REACH), 0, SLOTS + 1).astype(jnp.int32)
    base = jnp.clip(pick + hub[:, None] * SLOT_DEV, 0, SLOTS)
    low = offsets[None, :] < HOPS
    centre = offsets[None, :] == HOPS
    counts = jnp.where(low, base, jnp.where(centre, SLOTS, base[joined, mirror])).astype(jnp.int32)
    scores = jax.random.randint(jax.random.fold_in(key, 13), (GROUPS, REACH, combos), 0, 1 << 20).astype(jnp.int32)
    scores = scores * combos + jnp.arange(combos, dtype=jnp.int32)
    order = jnp.argsort(scores, axis=-1)[:, :, :SLOTS].astype(jnp.int32)
    first = order // BLK
    second = order % BLK
    slot = jnp.arange(SLOTS, dtype=jnp.int32)
    odd = (slot % 2 == 1)[None, None, :]
    half_first = first[:, :, slot // 2]
    half_second = second[:, :, slot // 2]
    diag_row = jnp.where(odd, half_second, half_first)
    diag_col = jnp.where(odd, half_first, half_second)
    row_coord = jnp.where(low[:, :, None], first, jnp.where(centre[:, :, None], diag_row, second[joined, mirror]))
    col_coord = jnp.where(low[:, :, None], second, jnp.where(centre[:, :, None], diag_col, first[joined, mirror]))
    return (counts, jnp.stack([row_coord, col_coord]).astype(jnp.int32))


def draw_tile_counts(key, part):
    counts, coords = pair_layout(key)
    return counts


def draw_tile_coords(key, part):
    counts, coords = pair_layout(key)
    return coords


def draw_tile_values(key, part):
    shape = (GROUPS, REACH, SLOTS, TILE, TILE)
    raw = jnp.clip(jax.random.normal(jax.random.fold_in(key, 21), shape, jnp.float32), -6.0, 6.0)
    joined, mirror, offsets = partner_index()
    low = (offsets < HOPS)[None, :, None, None, None]
    centre = (offsets == HOPS)[None, :, None, None, None]
    mirrored = jnp.swapaxes(raw[joined, mirror], 3, 4)
    slot = jnp.arange(SLOTS, dtype=jnp.int32)
    odd = (slot % 2 == 1)[None, None, :, None, None]
    paired = raw[:, :, slot - slot % 2]
    diag = jnp.where(odd, jnp.swapaxes(paired, 3, 4), paired)
    sym = jnp.where(low, raw, jnp.where(centre, diag, mirrored))
    return (sym * (REACH * SLOTS * TILE // BLK) ** (-0.5)).astype(jnp.bfloat16)


def steps_of(stream_key, shape, split, smallest, largest):
    def one(dim, parts):
        draws = jax.random.uniform(jax.random.fold_in(jax.random.fold_in(stream_key, 6), dim), (parts,), jnp.float32, smallest / len(split), largest / len(split))
        return jnp.repeat(jnp.exp(draws), shape[dim] // parts).reshape((-1,) + (1,) * (len(shape) - dim - 1))

    level = one(*split[0])
    for cut in split[1:]:
        level = level * one(*cut)
    return level


def normal_values(stream_key, dims, scale, most, cuts=(), kind=jnp.bfloat16):
    drawn = jax.random.normal(stream_key, dims, jnp.float32) * scale
    if len(cuts) > 0:
        drawn = steps_of(stream_key, dims, cuts, -0.22, 0.18) * drawn
    return jnp.clip(drawn, min=-most, max=most).astype(kind)


def setup_inputs(seed: int = 0) -> dict:
    streams_of = jax.random.split(jax.random.key(seed), 7)
    return {
        "node_feats": normal_values(streams_of[0], (NODES, F), 1.0, 6.0, ((0, 128),)),
        "weight": normal_values(streams_of[1], (F, F), F ** -0.5, 0.375),
        "cotangent": normal_values(streams_of[2], (NODES, F), 1.0, 6.0, ((0, 128),)),
        "tile_values": draw_tile_values(jax.random.fold_in(streams_of[6], 71), 0),
        "tile_coords": draw_tile_coords(jax.random.fold_in(streams_of[6], 71), 0),
        "tile_counts": draw_tile_counts(jax.random.fold_in(streams_of[6], 71), 0),
    }


def silu_slope(value):
    sig = jax.nn.sigmoid(value)
    return sig * (1.0 + value * (1.0 - sig))


def propagate(tile_values, tile_coords, tile_counts, source):
    panels = source.reshape(GROUPS, BLK, TILE, F)
    group_ids = jnp.arange(GROUPS, dtype=jnp.int32)
    offsets = jnp.arange(REACH, dtype=jnp.int32)
    slot_ids = jnp.arange(SLOTS, dtype=jnp.int32)
    block_ids = jnp.arange(BLK, dtype=jnp.int32)

    def one_group(items):
        group, values_row, rows_row, cols_row, count_row = items
        joined = (group + offsets - HOPS) % GROUPS
        picked = panels[joined[:, None], cols_row.astype(jnp.int32)]
        product = jnp.einsum("dkuv,dkvf->dkuf", values_row.astype(jnp.float32), picked.astype(jnp.float32), precision=lax.Precision.HIGHEST)
        live = slot_ids[None, :] < count_row[:, None]
        place = ((rows_row[:, :, None] == block_ids[None, None, :]) & live[:, :, None]).astype(jnp.float32)
        return jnp.einsum("dkb,dkuf->buf", place, product, precision=lax.Precision.HIGHEST)

    summed = lax.map(one_group, (group_ids, tile_values, tile_coords[0], tile_coords[1], tile_counts))
    return summed.reshape(NODES, F)


def reference(node_feats, weight, cotangent, tile_values, tile_coords, tile_counts):
    transformed = jnp.dot(node_feats, weight, preferred_element_type=jnp.float32).astype(jnp.bfloat16)
    aggregated = propagate(tile_values, tile_coords, tile_counts, transformed)
    activated = jax.nn.silu(aggregated).astype(jnp.bfloat16)
    adjoint = (cotangent.astype(jnp.float32) * silu_slope(aggregated)).astype(jnp.bfloat16)
    back_sum = propagate(tile_values, tile_coords, tile_counts, adjoint).astype(jnp.bfloat16)
    weight_grad = jnp.dot(node_feats.T, back_sum, preferred_element_type=jnp.float32) * (NODES ** -0.5)
    input_grad = jnp.dot(back_sum, weight.T, preferred_element_type=jnp.float32).astype(jnp.bfloat16)
    return activated, input_grad, weight_grad
```

```python
import functools

import jax
import jax.numpy as jnp
from jax import lax
from jax.experimental import pallas as pl
from jax.experimental.pallas import tpu as pltpu
from jax.sharding import PartitionSpec as P

MESH = pl.DeviceIdType.MESH
BF16 = jnp.bfloat16
F32 = jnp.float32


def matmul(a, b):
    return jnp.dot(a, b, preferred_element_type=F32)


def layer_kernel(
    groups,
    reps,
    scale,
    x_hbm,
    w_ref,
    ct_hbm,
    tiles_hbm,
    coords_ref,
    counts_ref,
    act_hbm,
    ig_hbm,
    wg_ref,
    px,
    ad,
    dense,
    tl,
    tp,
    code,
    acc,
    send,
    ra,
    cb,
    rf,
    g,
    ctv,
    actv,
    xt,
    load_sem,
    out_sem,
    x_send,
    x_recv,
    a_send,
    a_recv,
    rs_send,
    rs_recv,
    ag_send,
    ag_recv,
):
    me = lax.axis_index("rows")
    p = lax.axis_index("rep")
    up, dn = lax.rem(me + 2, groups), lax.rem(me + groups - 2, groups)
    odd = lax.rem(me, 2)
    mate = me + 1 - 2 * odd
    nxt, prv, opp = (lax.rem(p + k, reps) for k in (1, reps - 1, 2))
    n, f = acc.shape
    q = n // reps
    h = q // 2
    reach, slots, tile, _ = tl.shape
    blocks = n // tile
    out_slot = 1 + 2 * odd
    mate_slot = 3 - 2 * odd
    fwd_slot = 4 - 4 * odd
    far_slot = 4 * odd

    def rows(start, size):
        return pl.ds(pl.multiple_of(start, h), size)

    def remote(src, dst, ssem, rsem, dev):
        return pltpu.make_async_remote_copy(
            src_ref=src, dst_ref=dst, send_sem=ssem, recv_sem=rsem, device_id=dev, device_id_type=MESH
        )

    barrier = pltpu.get_barrier_semaphore()
    for dev in ((up, p), (dn, p), (mate, p), (me, nxt), (me, prv)):
        pl.semaphore_signal(barrier, inc=1, device_id=dev, device_id_type=MESH)

    loads = [
        pltpu.make_async_copy(src, dst, load_sem.at[i])
        for i, (src, dst) in enumerate(((tiles_hbm, tl), (x_hbm, px.at[2]), (ct_hbm, ctv)))
    ]
    for load in loads:
        load.start()

    pl.semaphore_wait(barrier, 5)

    def panel_copy(src, dst, ssem, rsem, kind, chunk):
        part = rows(chunk * q, q)
        slot = (0, 4, out_slot, mate_slot)[kind]
        dev = ((up, p), (dn, p), (mate, p), (mate, p))[kind]
        source = dst.at[fwd_slot, part] if kind == 3 else src.at[part]
        return remote(source, dst.at[slot, part], ssem.at[kind, chunk], rsem.at[slot, chunk], dev)

    def panel_wait(dst, ssem, rsem, slot, chunk):
        part = dst.at[slot, rows(chunk * q, q)]
        remote(part, part, ssem.at[0, chunk], rsem.at[slot, chunk], (mate, p)).wait_recv()

    @pl.loop(0, reps)
    def _(i):
        for kind in range(3):
            panel_copy(x_hbm, px, x_send, x_recv, kind, i).start()

    first = p * slots

    @pl.loop(0, reach)
    def _(d):
        for k in range(slots):
            live = first + k < counts_ref[0, d]
            at = coords_ref[0, 0, d, k] * blocks + coords_ref[1, 0, d, k]
            code[d * slots + k] = jnp.where(live, at, -1)

    tp[reach * slots] = jnp.zeros((tile, tile), BF16)
    loads[0].wait()

    @pl.loop(0, reach * slots)
    def _(t):
        base = (t // slots) * slots
        mine = code[t]
        total = jnp.zeros((tile, tile), F32)
        for j in range(slots):
            same = jnp.where(code[base + j] == mine, 1.0, 0.0).astype(F32)
            total = total + same * tl[t // slots, j].astype(F32)
        tp[t] = total.astype(BF16)

    @pl.loop(0, reach * blocks)
    def _(t):
        d = t // blocks
        b = lax.rem(t, blocks)
        part = pl.ds(pl.multiple_of(b * tile, tile), tile)
        for c in range(blocks):
            found = jnp.int32(reach * slots)
            for k in range(slots):
                found = jnp.where(code[d * slots + k] == b * blocks + c, d * slots + k, found)
            width = q // tile
            dense[d, c // width, part, (c % width) * tile : (c % width + 1) * tile] = tp[found]

    loads[1].wait()
    w = w_ref[...]

    def absorb(slot, chunk, panel, init=False):
        @pl.loop(0, reps)
        def _(b):
            part = rows(b * q, q)
            term = matmul(dense[slot, chunk, part, :], panel)
            acc[part, :] = term if init else acc[part, :] + term

    def x_absorb(slot, chunk, init=False):
        absorb(slot, chunk, matmul(px[slot, rows(chunk * q, q), :], w).astype(BF16), init)

    x_absorb(2, 0, True)

    @pl.loop(1, reps)
    def _(i):
        x_absorb(2, i)

    @pl.loop(0, reps)
    def _(i):
        xt[:, rows(i * q, q)] = px[2, rows(i * q, q), :].T

    @pl.loop(0, reps)
    def _(i):
        panel_wait(px, x_send, x_recv, mate_slot, i)
        x_absorb(mate_slot, i)

    @pl.loop(0, reps)
    def _(i):
        panel_wait(px, x_send, x_recv, fwd_slot, i)
        panel_copy(x_hbm, px, x_send, x_recv, 3, i).start()
        x_absorb(fwd_slot, i)
        panel_wait(px, x_send, x_recv, far_slot, i)
        x_absorb(far_slot, i)
        panel_wait(px, x_send, x_recv, out_slot, i)
        x_absorb(out_slot, i)

    sent = []

    def go(copy):
        copy.start()
        sent.append(copy)
        return copy

    def rs_start(ph):
        ssem, rsem = rs_send.at[ph], rs_recv.at[ph]
        buf = send.at[ph]

        def cast(part):
            buf[part, :] = acc[part, :].astype(BF16)

        cast(rows(opp * q, q))
        first_hop = [
            go(remote(buf.at[rows(opp * q, h)], ra.at[ph, 0], ssem.at[0], rsem.at[0], (me, nxt))),
            go(remote(buf.at[rows(opp * q + h, h)], ra.at[ph, 1], ssem.at[1], rsem.at[1], (me, prv))),
        ]
        cast(rows(nxt * q, q))
        cast(rows(prv * q, q))
        last_hop = [
            go(remote(buf.at[rows(nxt * q + h, h)], rf.at[ph, 0, pl.ds(h, h)], ssem.at[2], rsem.at[2], (me, nxt))),
            go(remote(buf.at[rows(prv * q, h)], rf.at[ph, 1, pl.ds(0, h)], ssem.at[3], rsem.at[3], (me, prv))),
        ]
        return first_hop, last_hop

    def rs_finish(ph, copies):
        ssem, rsem = rs_send.at[ph], rs_recv.at[ph]
        first_hop, last_hop = copies
        for k, (start, dev) in enumerate(((nxt * q, nxt), (prv * q + h, prv))):
            first_hop[k].wait_recv()
            cb[ph, k] = (ra[ph, k].astype(F32) + acc[rows(start, h), :]).astype(BF16)
            last_hop.append(
                go(remote(cb.at[ph, k], rf.at[ph, k, pl.ds(k * h, h)], ssem.at[4 + k], rsem.at[4 + k], (me, dev)))
            )
        for copy in last_hop:
            copy.wait_recv()
        return acc[rows(p * q, q), :] + rf[ph, 0].astype(F32) + rf[ph, 1].astype(F32)

    def ag_copy(ph, k, start, size, dev):
        part = g.at[ph, rows(start, size)]
        return remote(part, part, ag_send.at[ph, k], ag_recv.at[ph, k], (me, dev))

    def ag_start(ph):
        go(ag_copy(ph, 0, p * q, q, nxt))
        go(ag_copy(ph, 1, p * q, q, prv))

    def ag_pass(ph, k):
        if k == 0:
            ag_copy(ph, 0, prv * q, q, prv).wait_recv()
            go(ag_copy(ph, 2, prv * q, h, nxt))
        else:
            ag_copy(ph, 1, nxt * q, q, nxt).wait_recv()
            go(ag_copy(ph, 3, nxt * q + h, h, prv))

    def ag_last(ph):
        ag_copy(ph, 2, opp * q, h, prv).wait_recv()
        ag_copy(ph, 3, opp * q + h, h, nxt).wait_recv()

    def store_out(k, src, dst, start, size):
        part = rows(start, size)
        copy = pltpu.make_async_copy(src.at[part], dst.at[part], out_sem.at[k])
        copy.start()
        return copy

    outs = []

    g[0, rows(p * q, q), :] = rs_finish(0, rs_start(0)).astype(BF16)
    ag_start(0)
    loads[2].wait()

    def activate(k, at):
        part = rows(at * q, q)
        value = g[0, part, :].astype(F32)
        sig = jax.nn.sigmoid(value)
        ad[2, part, :] = (ctv[part, :].astype(F32) * (sig * (1.0 + value * (1.0 - sig)))).astype(BF16)
        for kind in range(3):
            panel_copy(ad.at[2], ad, a_send, a_recv, kind, at).start()
        actv[part, :] = (value * sig).astype(BF16)
        outs.append(store_out(k, actv, act_hbm, at * q, q))

    def a_absorb(slot, chunk, init=False):
        absorb(slot, chunk, ad[slot, rows(chunk * q, q), :], init)

    def a_round(at):
        panel_wait(ad, a_send, a_recv, fwd_slot, at)
        panel_copy(ad.at[2], ad, a_send, a_recv, 3, at).start()
        panel_wait(ad, a_send, a_recv, mate_slot, at)
        a_absorb(mate_slot, at)
        a_absorb(fwd_slot, at)
        panel_wait(ad, a_send, a_recv, far_slot, at)
        a_absorb(far_slot, at)
        panel_wait(ad, a_send, a_recv, out_slot, at)
        a_absorb(out_slot, at)

    activate(0, p)
    a_absorb(2, p, True)
    ag_pass(0, 0)
    activate(1, prv)
    ag_pass(0, 1)
    activate(2, nxt)
    a_absorb(2, prv)
    a_round(p)
    ag_last(0)
    activate(3, opp)
    a_absorb(2, nxt)
    a_absorb(2, opp)

    @pl.loop(0, reps - 1)
    def _(j):
        a_round(jnp.where(j == 0, prv, jnp.where(j == 1, nxt, opp)))

    copies = rs_start(1)
    send[1, rows(p * q, q), :] = acc[rows(p * q, q), :].astype(BF16)
    wg_ref[...] = matmul(xt[...], send[1]) * scale
    back = rs_finish(1, copies).astype(BF16)
    g[1, rows(p * q, q), :] = lax.dot_general(
        back, w, (((1,), (1,)), ((), ())), preferred_element_type=F32
    ).astype(BF16)
    ag_start(1)
    outs.append(store_out(4, g.at[1], ig_hbm, p * q, q))
    ag_pass(1, 0)
    outs.append(store_out(5, g.at[1], ig_hbm, prv * q, q))
    ag_pass(1, 1)
    outs.append(store_out(6, g.at[1], ig_hbm, nxt * q, q))
    ag_last(1)
    outs.append(store_out(7, g.at[1], ig_hbm, opp * q, q))

    for copy in sent:
        copy.wait_send()

    @pl.loop(0, reps)
    def _(i):
        for kind in range(4):
            panel_copy(x_hbm, px, x_send, x_recv, kind, i).wait_send()
            panel_copy(ad.at[2], ad, a_send, a_recv, kind, i).wait_send()

    for copy in outs:
        copy.wait()


def per_device(groups, reps, node_feats, weight, cotangent, tile_values, tile_coords, tile_counts):
    n, f = node_feats.shape
    _, reach, slots, tile, _ = tile_values.shape
    q = n // reps
    h = q // 2
    dma = pltpu.SemaphoreType.DMA
    hbm = pl.BlockSpec(memory_space=pl.ANY)
    vmem = pl.BlockSpec(memory_space=pltpu.VMEM)
    smem = pl.BlockSpec(memory_space=pltpu.SMEM)
    activated, input_grad, grad_terms = pl.pallas_call(
        functools.partial(layer_kernel, groups, reps, (n * groups) ** (-0.5)),
        out_shape=(
            jax.ShapeDtypeStruct((n, f), BF16),
            jax.ShapeDtypeStruct((n, f), BF16),
            jax.ShapeDtypeStruct((f, f), F32),
        ),
        in_specs=[hbm, vmem, hbm, hbm, smem, smem],
        out_specs=(hbm, hbm, vmem),
        scratch_shapes=[
            pltpu.VMEM((reach, n, f), BF16),
            pltpu.VMEM((reach, n, f), BF16),
            pltpu.VMEM((reach, reps, n, q), BF16),
            pltpu.VMEM((reach, slots, tile, tile), BF16),
            pltpu.VMEM((reach * slots + 1, tile, tile), BF16),
            pltpu.SMEM((reach * slots,), jnp.int32),
            pltpu.VMEM((n, f), F32),
            pltpu.VMEM((2, n, f), BF16),
            pltpu.VMEM((2, 2, h, f), BF16),
            pltpu.VMEM((2, 2, h, f), BF16),
            pltpu.VMEM((2, 2, q, f), BF16),
            pltpu.VMEM((2, n, f), BF16),
            pltpu.VMEM((n, f), BF16),
            pltpu.VMEM((n, f), BF16),
            pltpu.VMEM((f, n), BF16),
            dma((3,)),
            dma((8,)),
            dma((4, reps)),
            dma((reach, reps)),
            dma((4, reps)),
            dma((reach, reps)),
            dma((2, 6)),
            dma((2, 6)),
            dma((2, 4)),
            dma((2, 4)),
        ],
        compiler_params=pltpu.CompilerParams(
            collective_id=0, has_side_effects=True, vmem_limit_bytes=56 << 20
        ),
    )(node_feats, weight, cotangent, tile_values[0], tile_coords, tile_counts)
    weight_grad = lax.psum(grad_terms, ("rows", "rep"))
    return (activated, input_grad, weight_grad)


def solution(mesh):
    return jax.shard_map(
        functools.partial(per_device, mesh.shape["rows"], mesh.shape["rep"]),
        mesh=mesh,
        in_specs=(
            P("rows", None),
            P(),
            P("rows", None),
            P("rows", None, "rep", None, None),
            P(None, "rows", None, "rep"),
            P("rows", None),
        ),
        out_specs=(P("rows", None), P("rows", None), P()),
        check_vma=False,
    )
```

```python
import functools

import jax
import jax.numpy as jnp
from jax import lax
from jax.experimental import pallas as pl
from jax.experimental.pallas import tpu as pltpu
from jax.sharding import PartitionSpec as P

MESH = pl.DeviceIdType.MESH
BF16 = jnp.bfloat16
F32 = jnp.float32
ZS, XS, YL = 8, 4, 2


def matmul(a, b):
    return jnp.dot(a, b, preferred_element_type=F32)


def layer_kernel(
    groups,
    reps,
    scale,
    x_hbm,
    w_ref,
    ct_hbm,
    tiles_hbm,
    coords_ref,
    counts_ref,
    act_hbm,
    ig_hbm,
    wg_hbm,
    px,
    ad,
    dense,
    tl,
    tp,
    code,
    acc,
    send,
    ra,
    cb,
    rf,
    g,
    ctv,
    actv,
    v,
    xt,
    ws,
    w0,
    w1s,
    w1,
    w2,
    w3,
    wf,
    wp,
    w1f,
    load_sem,
    out_sem,
    x_send,
    x_recv,
    a_send,
    a_recv,
    rs_send,
    rs_recv,
    ag_send,
    ag_recv,
    w_send,
    w_recv,
):
    me = lax.axis_index("rows")
    p = lax.axis_index("rep")
    up, dn = lax.rem(me + 2, groups), lax.rem(me + groups - 2, groups)
    odd = lax.rem(me, 2)
    mate = me + 1 - 2 * odd
    nxt, prv, opp = (lax.rem(p + k, reps) for k in (1, reps - 1, 2))
    n, f = acc.shape
    q = n // reps
    h = q // 2
    reach, slots, tile, _ = tl.shape
    blocks = n // tile
    out_slot = 1 + 2 * odd
    mate_slot = 3 - 2 * odd
    fwd_slot = 4 - 4 * odd
    far_slot = 4 * odd

    def rows(start, size):
        return pl.ds(pl.multiple_of(start, h), size)

    def remote(src, dst, ssem, rsem, dev):
        return pltpu.make_async_remote_copy(
            src_ref=src, dst_ref=dst, send_sem=ssem, recv_sem=rsem, device_id=dev, device_id_type=MESH
        )

    z = lax.rem(me // 2, ZS)
    x = lax.rem(me // (2 * ZS), XS)
    y_lo = me // (2 * ZS * XS)
    y = p * YL + y_lo

    def z_peer(k):
        other = lax.rem(z + k, ZS)
        return other, (me + 2 * (other - z), p)

    def x_peer(k):
        other = lax.rem(x + k, XS)
        return other, (me + 2 * ZS * (other - x), p)

    def y_peer(k):
        other = lax.rem(y + k, YL * reps)
        return other, (me + 2 * ZS * XS * (lax.rem(other, YL) - y_lo), other // YL)

    z_peers = [z_peer(k) for k in range(1, ZS)]
    x_peers = [x_peer(k) for k in range(1, XS)]
    y_peers = [y_peer(k) for k in range(1, YL * reps)]
    greet = [(up, p), (dn, p), (mate, p)] + [dev for _, dev in z_peers + x_peers + y_peers]

    barrier = pltpu.get_barrier_semaphore()
    for dev in greet:
        pl.semaphore_signal(barrier, inc=1, device_id=dev, device_id_type=MESH)

    loads = [
        pltpu.make_async_copy(src, dst, load_sem.at[i])
        for i, (src, dst) in enumerate(((tiles_hbm, tl), (x_hbm, px.at[2]), (ct_hbm, ctv)))
    ]
    for load in loads:
        load.start()

    pl.semaphore_wait(barrier, len(greet))

    def panel_copy(src, dst, ssem, rsem, kind, chunk, size):
        part = rows(chunk * size, size)
        slot = (0, 4, out_slot, mate_slot)[kind]
        dev = ((up, p), (dn, p), (mate, p), (mate, p))[kind]
        source = dst.at[fwd_slot, part] if kind == 3 else src.at[part]
        return remote(source, dst.at[slot, part], ssem.at[kind, chunk], rsem.at[slot, chunk], dev)

    def panel_wait(dst, ssem, rsem, slot, chunk, size):
        part = dst.at[slot, rows(chunk * size, size)]
        remote(part, part, ssem.at[0, chunk], rsem.at[slot, chunk], (mate, p)).wait_recv()

    def x_copy(kind, chunk):
        return panel_copy(x_hbm, px, x_send, x_recv, kind, chunk, q)

    def x_wait(slot, chunk):
        panel_wait(px, x_send, x_recv, slot, chunk, q)

    def a_copy(kind, chunk):
        return panel_copy(ad.at[2], ad, a_send, a_recv, kind, chunk, h)

    def a_wait(slot, at):
        panel_wait(ad, a_send, a_recv, slot, 2 * at, h)
        panel_wait(ad, a_send, a_recv, slot, 2 * at + 1, h)

    def x_forward(chunk):
        x_wait(fwd_slot, chunk)
        x_copy(3, chunk).start()

    def a_forward(chunk):
        panel_wait(ad, a_send, a_recv, fwd_slot, chunk, h)
        a_copy(3, chunk).start()

    @pl.loop(0, reps)
    def _(i):
        for kind in range(3):
            x_copy(kind, i).start()

    first = p * slots

    @pl.loop(0, reach)
    def _(d):
        for k in range(slots):
            live = first + k < counts_ref[0, d]
            at = coords_ref[0, 0, d, k] * blocks + coords_ref[1, 0, d, k]
            code[d * slots + k] = jnp.where(live, at, -1)

    tp[reach * slots] = jnp.zeros((tile, tile), BF16)
    loads[0].wait()

    @pl.loop(0, reach)
    def _(d):
        for k in range(slots):
            total = tl[d, k].astype(F32)
            for j in range(k + 1, slots):
                same = jnp.where(code[d * slots + j] == code[d * slots + k], 1.0, 0.0).astype(F32)
                total = total + same * tl[d, j].astype(F32)
            tp[d * slots + k] = total.astype(BF16)

    @pl.loop(0, reach * blocks)
    def _(t):
        d = t // blocks
        b = lax.rem(t, blocks)
        part = pl.ds(pl.multiple_of(b * tile, tile), tile)
        for c in range(blocks):
            found = jnp.int32(reach * slots)
            for k in range(slots - 1, -1, -1):
                found = jnp.where(code[d * slots + k] == b * blocks + c, d * slots + k, found)
            width = q // tile
            dense[d, c // width, part, (c % width) * tile : (c % width + 1) * tile] = tp[found]

    loads[1].wait()
    w = w_ref[...]

    sent = []

    def go(copy):
        copy.start()
        sent.append(copy)
        return copy

    def absorb(slot, chunk, panel, init=False):
        term = matmul(dense[slot, chunk], panel)
        acc[...] = term if init else acc[...] + term

    def x_panel(slot, chunk):
        return matmul(px[slot, rows(chunk * q, q), :], w).astype(BF16)

    def x_whole(slot, init=False):
        for i in range(reps):
            v[pl.ds(i * q, q), :] = x_panel(slot, i)
        total = None if init else acc[...]
        for i in range(reps):
            term = matmul(dense[slot, i], v[pl.ds(i * q, q), :])
            total = term if total is None else total + term
        acc[...] = total

    def rs_start(ph, chunk, panels):
        ssem, rsem = rs_send.at[ph], rs_recv.at[ph]
        buf = send.at[ph]

        def block(at):
            part = rows(at * q, q)
            total = acc[part, :]
            for slot, panel in panels:
                total = total + matmul(dense[slot, chunk, part, :], panel())
            acc[part, :] = total
            buf[part, :] = total.astype(BF16)

        block(opp)
        first_hop = [
            go(remote(buf.at[rows(opp * q, h)], ra.at[ph, 0], ssem.at[0], rsem.at[0], (me, nxt))),
            go(remote(buf.at[rows(opp * q + h, h)], ra.at[ph, 1], ssem.at[1], rsem.at[1], (me, prv))),
        ]
        block(nxt)
        last_hop = [
            go(remote(buf.at[rows(nxt * q + h, h)], rf.at[ph, 0, pl.ds(h, h)], ssem.at[2], rsem.at[2], (me, nxt))),
        ]
        block(prv)
        last_hop.append(
            go(remote(buf.at[rows(prv * q, h)], rf.at[ph, 1, pl.ds(0, h)], ssem.at[3], rsem.at[3], (me, prv)))
        )
        block(p)
        return first_hop, last_hop

    x_whole(2, True)
    x_forward(0)

    @pl.loop(0, reps)
    def _(i):
        x_wait(mate_slot, i)

    x_whole(mate_slot)

    @pl.loop(0, reps)
    def _(i):
        xt[:, rows(i * q, q)] = px[2, rows(i * q, q), :].T

    @pl.loop(0, reps - 1)
    def _(i):
        absorb(fwd_slot, i, x_panel(fwd_slot, i))
        x_wait(far_slot, i)
        absorb(far_slot, i, x_panel(far_slot, i))
        x_forward(i + 1)
        x_wait(out_slot, i)
        absorb(out_slot, i, x_panel(out_slot, i))

    last = reps - 1
    v[pl.ds(0, q), :] = x_panel(fwd_slot, last)
    x_wait(far_slot, last)
    v[pl.ds(q, q), :] = x_panel(far_slot, last)
    x_wait(out_slot, last)
    v[pl.ds(2 * q, q), :] = x_panel(out_slot, last)
    x_last = [
        (fwd_slot, lambda: v[pl.ds(0, q), :]),
        (far_slot, lambda: v[pl.ds(q, q), :]),
        (out_slot, lambda: v[pl.ds(2 * q, q), :]),
    ]

    def rs_middle(ph, copies):
        ssem, rsem = rs_send.at[ph], rs_recv.at[ph]
        first_hop, last_hop = copies
        for k, (start, dev) in enumerate(((nxt * q, nxt), (prv * q + h, prv))):
            first_hop[k].wait_recv()
            cb[ph, k] = (ra[ph, k].astype(F32) + acc[rows(start, h), :]).astype(BF16)
            last_hop.append(
                go(remote(cb.at[ph, k], rf.at[ph, k, pl.ds(k * h, h)], ssem.at[4 + k], rsem.at[4 + k], (me, dev)))
            )
        return last_hop

    def rs_finish(ph, last_hop):
        for copy in last_hop:
            copy.wait_recv()
        return acc[rows(p * q, q), :] + rf[ph, 0].astype(F32) + rf[ph, 1].astype(F32)

    def ag_copy(ph, k, at, half, dev):
        part = g.at[ph, rows(at * q + half * h, h)]
        return remote(part, part, ag_send.at[ph, k], ag_recv.at[ph, k], (me, dev))

    def ag_start(ph):
        go(ag_copy(ph, 0, p, 0, nxt))
        go(ag_copy(ph, 1, p, 1, prv))
        go(ag_copy(ph, 2, p, 1, nxt))
        go(ag_copy(ph, 3, p, 0, prv))

    def ag_wait(ph, k):
        at, half = ((prv, 0), (nxt, 1), (prv, 1), (nxt, 0), (opp, 0), (opp, 1))[k]
        ag_copy(ph, k, at, half, prv).wait_recv()
        if k < 2:
            go(ag_copy(ph, 4 + k, at, half, (nxt, prv)[k]))

    def store_out(k, src, dst, start, size):
        part = rows(start, size)
        copy = pltpu.make_async_copy(src.at[part], dst.at[part], out_sem.at[k])
        copy.start()
        return copy

    outs = []

    g[0, rows(p * q, q), :] = rs_finish(0, rs_middle(0, rs_start(0, last, x_last))).astype(BF16)
    ag_start(0)
    loads[2].wait()

    def activate(at, half):
        start = at * q + half * h
        part = rows(start, h)
        value = g[0, part, :].astype(F32)
        sig = jax.nn.sigmoid(value)
        ad[2, part, :] = (ctv[part, :].astype(F32) * (sig * (1.0 + value * (1.0 - sig)))).astype(BF16)
        for kind in range(3):
            a_copy(kind, 2 * at + half).start()
        actv[part, :] = (value * sig).astype(BF16)
        outs.append(store_out(len(outs), actv, act_hbm, start, h))

    def a_panel(slot, chunk):
        return ad[slot, rows(chunk * q, q), :]

    activate(p, 0)
    activate(p, 1)
    absorb(2, p, a_panel(2, p), True)
    ag_wait(0, 0)
    activate(prv, 0)
    ag_wait(0, 1)
    activate(nxt, 1)
    a_forward(2 * p)
    a_forward(2 * p + 1)
    ag_wait(0, 2)
    activate(prv, 1)
    ag_wait(0, 3)
    activate(nxt, 0)
    a_wait(mate_slot, p)
    absorb(mate_slot, p, a_panel(mate_slot, p))
    absorb(fwd_slot, p, a_panel(fwd_slot, p))
    ag_wait(0, 4)
    activate(opp, 0)
    ag_wait(0, 5)
    activate(opp, 1)
    a_forward(2 * prv)
    a_forward(2 * nxt + 1)
    a_wait(far_slot, p)
    a_wait(out_slot, p)

    @pl.loop(0, 2)
    def _(i):
        slot = jnp.where(i == 0, far_slot, out_slot)
        absorb(slot, p, a_panel(slot, p))

    a_forward(2 * prv + 1)
    a_forward(2 * nxt)
    for at in (prv, nxt, opp):
        a_wait(mate_slot, at)

    @pl.loop(0, 6)
    def _(i):
        at = jnp.where(i // 2 == 0, prv, jnp.where(i // 2 == 1, nxt, opp))
        slot = jnp.where(lax.rem(i, 2) == 0, 2, mate_slot)
        absorb(slot, at, a_panel(slot, at))

    for at in (prv, nxt):
        a_wait(far_slot, at)
        a_wait(out_slot, at)

    @pl.loop(0, 6)
    def _(i):
        at = jnp.where(i < 3, prv, nxt)
        turn = lax.rem(i, 3)
        slot = jnp.where(turn == 0, fwd_slot, jnp.where(turn == 1, far_slot, out_slot))
        absorb(slot, at, a_panel(slot, at))

    a_forward(2 * opp)
    a_forward(2 * opp + 1)
    a_wait(far_slot, opp)
    a_wait(out_slot, opp)
    a_last = [(slot, functools.partial(a_panel, slot, opp)) for slot in (fwd_slot, far_slot, out_slot)]

    def w_go(step, to, src, dst, slot, dev):
        go(remote(src, dst, w_send.at[step, to], w_recv.at[step, slot], dev))

    def w_wait(step, ref, slot):
        remote(ref, ref, w_send.at[step, 0], w_recv.at[step, slot], (mate, p)).wait_recv()

    half, piece = f // 2, f // (2 * ZS)

    copies = rs_start(1, opp, a_last)
    terms = matmul(xt[...], send[1]) * scale
    wp[...] = terms
    ws[...] = terms.astype(BF16)
    w_go(0, 0, ws.at[rows((1 - odd) * half, half)], w0, 0, (mate, p))
    last_hop = rs_middle(1, copies)
    w_wait(0, w0, 0)
    mine = wp[rows(odd * half, half), :] + w0[...].astype(F32)
    w1f[...] = mine.reshape(ZS, piece, f)
    w1s[...] = w1f[...].astype(BF16)
    for other, dev in z_peers:
        w_go(1, other, w1s.at[other], w1.at[z], z, dev)
    part = w1f[z]
    for other, dev in z_peers:
        w_wait(1, w1.at[other], other)
        part = part + w1[other].astype(F32)
    w2[x] = part.astype(BF16)
    for other, dev in x_peers:
        w_go(2, other, w2.at[x], w2.at[x], x, dev)
    back = rs_finish(1, last_hop).astype(BF16)
    g[1, rows(p * q, q), :] = lax.dot_general(
        back, w, (((1,), (1,)), ((), ())), preferred_element_type=F32
    ).astype(BF16)
    ag_start(1)
    outs.append(store_out(len(outs), g.at[1], ig_hbm, p * q, q))
    for other, dev in x_peers:
        w_wait(2, w2.at[other], other)
    w3[y] = sum(w2[k].astype(F32) for k in range(XS)).astype(BF16)
    for other, dev in y_peers:
        w_go(3, other, w3.at[y], w3.at[y], y, dev)
    ag_wait(1, 0)
    ag_wait(1, 1)
    ag_wait(1, 2)
    outs.append(store_out(len(outs), g.at[1], ig_hbm, prv * q, q))
    ag_wait(1, 3)
    outs.append(store_out(len(outs), g.at[1], ig_hbm, nxt * q, q))
    for other, dev in y_peers:
        w_wait(3, w3.at[other], other)
    wf[odd, z] = sum(w3[k].astype(F32) for k in range(YL * reps))
    for other, dev in z_peers:
        w_go(4, other, wf.at[odd, z], wf.at[odd, z], z, dev)
    ag_wait(1, 4)
    ag_wait(1, 5)
    outs.append(store_out(len(outs), g.at[1], ig_hbm, opp * q, q))
    for other, dev in z_peers:
        w_wait(4, wf.at[odd, other], other)
    w_go(5, 0, wf.at[odd], wf.at[odd], 0, (mate, p))
    w_wait(5, wf.at[1 - odd], 0)
    copy = pltpu.make_async_copy(wf, wg_hbm, out_sem.at[len(outs)])
    copy.start()
    outs.append(copy)

    for copy in sent:
        copy.wait_send()

    @pl.loop(0, reps)
    def _(i):
        for kind in range(4):
            x_copy(kind, i).wait_send()

    @pl.loop(0, 2 * reps)
    def _(i):
        for kind in range(4):
            a_copy(kind, i).wait_send()

    for copy in outs:
        copy.wait()


def per_device(groups, reps, node_feats, weight, cotangent, tile_values, tile_coords, tile_counts):
    n, f = node_feats.shape
    _, reach, slots, tile, _ = tile_values.shape
    q = n // reps
    h = q // 2
    dma = pltpu.SemaphoreType.DMA
    piece = f // (2 * ZS)
    hbm = pl.BlockSpec(memory_space=pl.ANY)
    vmem = pl.BlockSpec(memory_space=pltpu.VMEM)
    smem = pl.BlockSpec(memory_space=pltpu.SMEM)
    activated, input_grad, weight_grad = pl.pallas_call(
        functools.partial(layer_kernel, groups, reps, (n * groups) ** (-0.5)),
        out_shape=(
            jax.ShapeDtypeStruct((n, f), BF16),
            jax.ShapeDtypeStruct((n, f), BF16),
            jax.ShapeDtypeStruct((2, ZS, piece, f), F32),
        ),
        in_specs=[hbm, vmem, hbm, hbm, smem, smem],
        out_specs=(hbm, hbm, hbm),
        scratch_shapes=[
            pltpu.VMEM((reach, n, f), BF16),
            pltpu.VMEM((reach, n, f), BF16),
            pltpu.VMEM((reach, reps, n, q), BF16),
            pltpu.VMEM((reach, slots, tile, tile), BF16),
            pltpu.VMEM((reach * slots + 1, tile, tile), BF16),
            pltpu.SMEM((reach * slots,), jnp.int32),
            pltpu.VMEM((n, f), F32),
            pltpu.VMEM((2, n, f), BF16),
            pltpu.VMEM((2, 2, h, f), BF16),
            pltpu.VMEM((2, 2, h, f), BF16),
            pltpu.VMEM((2, 2, q, f), BF16),
            pltpu.VMEM((2, n, f), BF16),
            pltpu.VMEM((n, f), BF16),
            pltpu.VMEM((n, f), BF16),
            pltpu.VMEM((n, f), BF16),
            pltpu.VMEM((f, n), BF16),
            pltpu.VMEM((f, f), BF16),
            pltpu.VMEM((f // 2, f), BF16),
            pltpu.VMEM((ZS, piece, f), BF16),
            pltpu.VMEM((ZS, piece, f), BF16),
            pltpu.VMEM((XS, piece, f), BF16),
            pltpu.VMEM((YL * reps, piece, f), BF16),
            pltpu.VMEM((2, ZS, piece, f), F32),
            pltpu.VMEM((f, f), F32),
            pltpu.VMEM((ZS, piece, f), F32),
            dma((3,)),
            dma((16,)),
            dma((4, reps)),
            dma((reach, reps)),
            dma((4, 2 * reps)),
            dma((reach, 2 * reps)),
            dma((2, 6)),
            dma((2, 6)),
            dma((2, 6)),
            dma((2, 6)),
            dma((6, 8)),
            dma((6, 8)),
        ],
        compiler_params=pltpu.CompilerParams(
            collective_id=0, vmem_limit_bytes=56 << 20
        ),
    )(node_feats, weight, cotangent, tile_values[0], tile_coords, tile_counts)
    return (activated, input_grad, weight_grad.reshape(f, f))


def solution(mesh):
    return jax.shard_map(
        functools.partial(per_device, mesh.shape["rows"], mesh.shape["rep"]),
        mesh=mesh,
        in_specs=(
            P("rows", None),
            P(),
            P("rows", None),
            P("rows", None, "rep", None, None),
            P(None, "rows", None, "rep"),
            P("rows", None),
        ),
        out_specs=(P("rows", None), P("rows", None), P()),
        check_vma=False,
    )
```

```python
import functools

import jax
import jax.numpy as jnp
from jax import lax
from jax.experimental import pallas as pl
from jax.experimental.pallas import tpu as pltpu
from jax.sharding import PartitionSpec as P

MESH = pl.DeviceIdType.MESH
BF16 = jnp.bfloat16
F32 = jnp.float32
ZS, XS, YL = 8, 4, 2


def matmul(a, b):
    return jnp.dot(a, b, preferred_element_type=F32)


def layer_kernel(
    groups,
    reps,
    scale,
    x_hbm,
    w_ref,
    ct_hbm,
    tiles_hbm,
    coords_ref,
    counts_ref,
    act_hbm,
    ig_hbm,
    wg_hbm,
    px,
    ad,
    dense,
    tl,
    tp,
    code,
    acc,
    send,
    ra,
    cb,
    rf,
    g,
    ctv,
    actv,
    v,
    xt,
    ws,
    w1,
    w2,
    w3,
    wf,
    wp,
    load_sem,
    out_sem,
    x_send,
    x_recv,
    a_send,
    a_recv,
    rs_send,
    rs_recv,
    ag_send,
    ag_recv,
    w_send,
    w_recv,
):
    me = lax.axis_index("rows")
    p = lax.axis_index("rep")
    up, dn = lax.rem(me + 2, groups), lax.rem(me + groups - 2, groups)
    odd = lax.rem(me, 2)
    mate = me + 1 - 2 * odd
    nxt, prv, opp = (lax.rem(p + k, reps) for k in (1, reps - 1, 2))
    n, f = acc.shape
    q = n // reps
    h = q // 2
    reach, slots, tile, _ = tl.shape
    blocks = n // tile
    out_slot = 1 + 2 * odd
    mate_slot = 3 - 2 * odd
    fwd_slot = 4 - 4 * odd
    far_slot = 4 * odd

    def rows(start, size):
        return pl.ds(pl.multiple_of(start, h), size)

    def remote(src, dst, ssem, rsem, dev):
        return pltpu.make_async_remote_copy(
            src_ref=src, dst_ref=dst, send_sem=ssem, recv_sem=rsem, device_id=dev, device_id_type=MESH
        )

    z = lax.rem(me // 2, ZS)
    x = lax.rem(me // (2 * ZS), XS)
    y_lo = me // (2 * ZS * XS)
    y = p * YL + y_lo

    def z_peer(k, core):
        other = lax.rem(z + k, ZS)
        return core * ZS + other, (me + 2 * (other - z) + core - odd, p)

    def x_peer(k):
        other = lax.rem(x + k, XS)
        return other, (me + 2 * ZS * (other - x), p)

    def y_peer(k):
        other = lax.rem(y + k, YL * reps)
        return other, (me + 2 * ZS * XS * (lax.rem(other, YL) - y_lo), other // YL)

    z_peers = [z_peer(k, core) for k in range(1, ZS) for core in range(2)]
    z_peers.append(((1 - odd) * ZS + z, (mate, p)))
    spot = odd * ZS + z
    x_peers = [x_peer(k) for k in range(1, XS)]
    y_peers = [y_peer(k) for k in range(1, YL * reps)]
    greet = [(up, p), (dn, p)] + [dev for _, dev in z_peers + x_peers + y_peers]

    barrier = pltpu.get_barrier_semaphore()
    for dev in greet:
        pl.semaphore_signal(barrier, inc=1, device_id=dev, device_id_type=MESH)

    loads = [
        pltpu.make_async_copy(src, dst, load_sem.at[i])
        for i, (src, dst) in enumerate(((tiles_hbm, tl), (x_hbm, px.at[2]), (ct_hbm, ctv)))
    ]
    for load in loads:
        load.start()

    pl.semaphore_wait(barrier, len(greet))

    def panel_copy(src, dst, ssem, rsem, kind, chunk, size):
        part = rows(chunk * size, size)
        slot = (0, 4, out_slot, mate_slot)[kind]
        dev = ((up, p), (dn, p), (mate, p), (mate, p))[kind]
        source = dst.at[fwd_slot, part] if kind == 3 else src.at[part]
        return remote(source, dst.at[slot, part], ssem.at[kind, chunk], rsem.at[slot, chunk], dev)

    def panel_wait(dst, ssem, rsem, slot, chunk, size):
        part = dst.at[slot, rows(chunk * size, size)]
        remote(part, part, ssem.at[0, chunk], rsem.at[slot, chunk], (mate, p)).wait_recv()

    def x_copy(kind, chunk):
        return panel_copy(x_hbm, px, x_send, x_recv, kind, chunk, q)

    def x_wait(slot, chunk):
        panel_wait(px, x_send, x_recv, slot, chunk, q)

    def a_copy(kind, chunk):
        return panel_copy(ad.at[2], ad, a_send, a_recv, kind, chunk, h)

    def a_wait(slot, at):
        panel_wait(ad, a_send, a_recv, slot, 2 * at, h)
        panel_wait(ad, a_send, a_recv, slot, 2 * at + 1, h)

    def x_forward(chunk):
        x_wait(fwd_slot, chunk)
        x_copy(3, chunk).start()

    def a_forward(chunk):
        panel_wait(ad, a_send, a_recv, fwd_slot, chunk, h)
        a_copy(3, chunk).start()

    @pl.loop(0, reps)
    def _(i):
        for kind in range(3):
            x_copy(kind, i).start()

    first = p * slots

    @pl.loop(0, reach)
    def _(d):
        for k in range(slots):
            live = first + k < counts_ref[0, d]
            at = coords_ref[0, 0, d, k] * blocks + coords_ref[1, 0, d, k]
            code[d * slots + k] = jnp.where(live, at, -1)

    tp[reach * slots] = jnp.zeros((tile, tile), BF16)
    loads[0].wait()

    @pl.loop(0, reach)
    def _(d):
        for k in range(slots):
            total = tl[d, k].astype(F32)
            for j in range(k + 1, slots):
                same = jnp.where(code[d * slots + j] == code[d * slots + k], 1.0, 0.0).astype(F32)
                total = total + same * tl[d, j].astype(F32)
            tp[d * slots + k] = total.astype(BF16)

    @pl.loop(0, reach * blocks)
    def _(t):
        d = t // blocks
        b = lax.rem(t, blocks)
        part = pl.ds(pl.multiple_of(b * tile, tile), tile)
        for c in range(blocks):
            found = jnp.int32(reach * slots)
            for k in range(slots - 1, -1, -1):
                found = jnp.where(code[d * slots + k] == b * blocks + c, d * slots + k, found)
            width = q // tile
            dense[d, c // width, part, (c % width) * tile : (c % width + 1) * tile] = tp[found]

    loads[1].wait()
    w = w_ref[...]

    sent = []

    def go(copy):
        copy.start()
        sent.append(copy)
        return copy

    def absorb(slot, chunk, panel, init=False):
        term = matmul(dense[slot, chunk], panel)
        acc[...] = term if init else acc[...] + term

    def x_panel(slot, chunk):
        return matmul(px[slot, rows(chunk * q, q), :], w).astype(BF16)

    def x_whole(slot, init=False):
        for i in range(reps):
            v[pl.ds(i * q, q), :] = x_panel(slot, i)
        total = None if init else acc[...]
        for i in range(reps):
            term = matmul(dense[slot, i], v[pl.ds(i * q, q), :])
            total = term if total is None else total + term
        acc[...] = total

    def rs_start(ph, chunk, panels):
        ssem, rsem = rs_send.at[ph], rs_recv.at[ph]
        buf = send.at[ph]

        def block(at):
            part = rows(at * q, q)
            total = acc[part, :]
            for slot, panel in panels:
                total = total + matmul(dense[slot, chunk, part, :], panel())
            acc[part, :] = total
            buf[part, :] = total.astype(BF16)

        block(opp)
        first_hop = [
            go(remote(buf.at[rows(opp * q, h)], ra.at[ph, 0], ssem.at[0], rsem.at[0], (me, nxt))),
            go(remote(buf.at[rows(opp * q + h, h)], ra.at[ph, 1], ssem.at[1], rsem.at[1], (me, prv))),
        ]
        block(nxt)
        last_hop = [
            go(remote(buf.at[rows(nxt * q + h, h)], rf.at[ph, 0, pl.ds(h, h)], ssem.at[2], rsem.at[2], (me, nxt))),
        ]
        block(prv)
        last_hop.append(
            go(remote(buf.at[rows(prv * q, h)], rf.at[ph, 1, pl.ds(0, h)], ssem.at[3], rsem.at[3], (me, prv)))
        )
        block(p)
        return first_hop, last_hop

    x_whole(2, True)
    x_forward(0)

    @pl.loop(0, reps)
    def _(i):
        x_wait(mate_slot, i)

    x_whole(mate_slot)

    @pl.loop(0, reps)
    def _(i):
        xt[:, rows(i * q, q)] = px[2, rows(i * q, q), :].T

    @pl.loop(0, reps - 1)
    def _(i):
        absorb(fwd_slot, i, x_panel(fwd_slot, i))
        x_wait(far_slot, i)
        absorb(far_slot, i, x_panel(far_slot, i))
        x_forward(i + 1)
        x_wait(out_slot, i)
        absorb(out_slot, i, x_panel(out_slot, i))

    last = reps - 1
    v[pl.ds(0, q), :] = x_panel(fwd_slot, last)
    x_wait(far_slot, last)
    v[pl.ds(q, q), :] = x_panel(far_slot, last)
    x_wait(out_slot, last)
    v[pl.ds(2 * q, q), :] = x_panel(out_slot, last)
    x_last = [
        (fwd_slot, lambda: v[pl.ds(0, q), :]),
        (far_slot, lambda: v[pl.ds(q, q), :]),
        (out_slot, lambda: v[pl.ds(2 * q, q), :]),
    ]

    def rs_middle(ph, copies):
        ssem, rsem = rs_send.at[ph], rs_recv.at[ph]
        first_hop, last_hop = copies
        for k, (start, dev) in enumerate(((nxt * q, nxt), (prv * q + h, prv))):
            first_hop[k].wait_recv()
            cb[ph, k] = (ra[ph, k].astype(F32) + acc[rows(start, h), :]).astype(BF16)
            last_hop.append(
                go(remote(cb.at[ph, k], rf.at[ph, k, pl.ds(k * h, h)], ssem.at[4 + k], rsem.at[4 + k], (me, dev)))
            )
        return last_hop

    def rs_finish(ph, last_hop):
        for copy in last_hop:
            copy.wait_recv()
        return acc[rows(p * q, q), :] + rf[ph, 0].astype(F32) + rf[ph, 1].astype(F32)

    def ag_copy(ph, k, at, half, dev):
        part = g.at[ph, rows(at * q + half * h, h)]
        return remote(part, part, ag_send.at[ph, k], ag_recv.at[ph, k], (me, dev))

    def ag_start(ph):
        go(ag_copy(ph, 0, p, 0, nxt))
        go(ag_copy(ph, 1, p, 1, prv))
        go(ag_copy(ph, 2, p, 1, nxt))
        go(ag_copy(ph, 3, p, 0, prv))

    def ag_wait(ph, k):
        at, half = ((prv, 0), (nxt, 1), (prv, 1), (nxt, 0), (opp, 0), (opp, 1))[k]
        ag_copy(ph, k, at, half, prv).wait_recv()
        if k < 2:
            go(ag_copy(ph, 4 + k, at, half, (nxt, prv)[k]))

    def store_out(k, src, dst, start, size):
        part = rows(start, size)
        copy = pltpu.make_async_copy(src.at[part], dst.at[part], out_sem.at[k])
        copy.start()
        return copy

    outs = []

    g[0, rows(p * q, q), :] = rs_finish(0, rs_middle(0, rs_start(0, last, x_last))).astype(BF16)
    ag_start(0)
    loads[2].wait()

    def activate(at, half):
        start = at * q + half * h
        part = rows(start, h)
        value = g[0, part, :].astype(F32)
        sig = jax.nn.sigmoid(value)
        ad[2, part, :] = (ctv[part, :].astype(F32) * (sig * (1.0 + value * (1.0 - sig)))).astype(BF16)
        for kind in range(3):
            a_copy(kind, 2 * at + half).start()
        actv[part, :] = (value * sig).astype(BF16)
        outs.append(store_out(len(outs), actv, act_hbm, start, h))

    def a_panel(slot, chunk):
        return ad[slot, rows(chunk * q, q), :]

    activate(p, 0)
    activate(p, 1)
    absorb(2, p, a_panel(2, p), True)
    ag_wait(0, 0)
    activate(prv, 0)
    ag_wait(0, 1)
    activate(nxt, 1)
    a_forward(2 * p)
    a_forward(2 * p + 1)
    ag_wait(0, 2)
    activate(prv, 1)
    ag_wait(0, 3)
    activate(nxt, 0)
    a_wait(mate_slot, p)
    absorb(mate_slot, p, a_panel(mate_slot, p))
    absorb(fwd_slot, p, a_panel(fwd_slot, p))
    ag_wait(0, 4)
    activate(opp, 0)
    ag_wait(0, 5)
    activate(opp, 1)
    a_forward(2 * prv)
    a_forward(2 * nxt + 1)
    a_wait(far_slot, p)
    a_wait(out_slot, p)

    @pl.loop(0, 2)
    def _(i):
        slot = jnp.where(i == 0, far_slot, out_slot)
        absorb(slot, p, a_panel(slot, p))

    a_forward(2 * prv + 1)
    a_forward(2 * nxt)
    for at in (prv, nxt, opp):
        a_wait(mate_slot, at)

    @pl.loop(0, 6)
    def _(i):
        at = jnp.where(i // 2 == 0, prv, jnp.where(i // 2 == 1, nxt, opp))
        slot = jnp.where(lax.rem(i, 2) == 0, 2, mate_slot)
        absorb(slot, at, a_panel(slot, at))

    for at in (prv, nxt):
        a_wait(far_slot, at)
        a_wait(out_slot, at)

    @pl.loop(0, 6)
    def _(i):
        at = jnp.where(i < 3, prv, nxt)
        turn = lax.rem(i, 3)
        slot = jnp.where(turn == 0, fwd_slot, jnp.where(turn == 1, far_slot, out_slot))
        absorb(slot, at, a_panel(slot, at))

    a_forward(2 * opp)
    a_forward(2 * opp + 1)
    a_wait(far_slot, opp)
    a_wait(out_slot, opp)
    a_last = [(slot, functools.partial(a_panel, slot, opp)) for slot in (fwd_slot, far_slot, out_slot)]

    def w_go(step, to, src, dst, slot, dev):
        go(remote(src, dst, w_send.at[step, to], w_recv.at[step, slot], dev))

    def w_wait(step, ref, slot):
        remote(ref, ref, w_send.at[step, 0], w_recv.at[step, slot], (mate, p)).wait_recv()

    copies = rs_start(1, opp, a_last)
    piece = f // (2 * ZS)
    wp[...] = (matmul(xt[...], send[1]) * scale).reshape(2 * ZS, piece, f)
    ws[...] = wp[...].astype(BF16)
    for other, dev in z_peers:
        w_go(0, other, ws.at[other], w1.at[spot], spot, dev)
    last_hop = rs_middle(1, copies)
    part = wp[spot]
    for other, dev in z_peers:
        w_wait(0, w1.at[other], other)
        part = part + w1[other].astype(F32)
    w2[x] = part.astype(BF16)
    for other, dev in x_peers:
        w_go(1, other, w2.at[x], w2.at[x], x, dev)
    for other, dev in x_peers:
        w_wait(1, w2.at[other], other)
    w3[y] = sum(w2[k].astype(F32) for k in range(XS)).astype(BF16)
    for other, dev in y_peers:
        w_go(2, other, w3.at[y], w3.at[y], y, dev)
    back = rs_finish(1, last_hop).astype(BF16)
    g[1, rows(p * q, q), :] = lax.dot_general(
        back, w, (((1,), (1,)), ((), ())), preferred_element_type=F32
    ).astype(BF16)
    ag_start(1)
    outs.append(store_out(len(outs), g.at[1], ig_hbm, p * q, q))
    ag_wait(1, 0)
    ag_wait(1, 1)
    for other, dev in y_peers:
        w_wait(2, w3.at[other], other)
    wf[spot] = sum(w3[k].astype(F32) for k in range(YL * reps)).astype(BF16)
    for other, dev in z_peers:
        w_go(3, other, wf.at[spot], wf.at[spot], spot, dev)
    ag_wait(1, 2)
    outs.append(store_out(len(outs), g.at[1], ig_hbm, prv * q, q))
    ag_wait(1, 3)
    outs.append(store_out(len(outs), g.at[1], ig_hbm, nxt * q, q))
    for other, dev in z_peers:
        w_wait(3, wf.at[other], other)
    wp[...] = wf[...].astype(F32)
    copy = pltpu.make_async_copy(wp, wg_hbm, out_sem.at[len(outs)])
    copy.start()
    outs.append(copy)
    ag_wait(1, 4)
    ag_wait(1, 5)
    outs.append(store_out(len(outs), g.at[1], ig_hbm, opp * q, q))

    for copy in sent:
        copy.wait_send()

    @pl.loop(0, reps)
    def _(i):
        for kind in range(4):
            x_copy(kind, i).wait_send()

    @pl.loop(0, 2 * reps)
    def _(i):
        for kind in range(4):
            a_copy(kind, i).wait_send()

    for copy in outs:
        copy.wait()


def per_device(groups, reps, node_feats, weight, cotangent, tile_values, tile_coords, tile_counts):
    n, f = node_feats.shape
    _, reach, slots, tile, _ = tile_values.shape
    q = n // reps
    h = q // 2
    dma = pltpu.SemaphoreType.DMA
    piece = f // (2 * ZS)
    hbm = pl.BlockSpec(memory_space=pl.ANY)
    vmem = pl.BlockSpec(memory_space=pltpu.VMEM)
    smem = pl.BlockSpec(memory_space=pltpu.SMEM)
    activated, input_grad, weight_grad = pl.pallas_call(
        functools.partial(layer_kernel, groups, reps, (n * groups) ** (-0.5)),
        out_shape=(
            jax.ShapeDtypeStruct((n, f), BF16),
            jax.ShapeDtypeStruct((n, f), BF16),
            jax.ShapeDtypeStruct((2 * ZS, piece, f), F32),
        ),
        in_specs=[hbm, vmem, hbm, hbm, smem, smem],
        out_specs=(hbm, hbm, hbm),
        scratch_shapes=[
            pltpu.VMEM((reach, n, f), BF16),
            pltpu.VMEM((reach, n, f), BF16),
            pltpu.VMEM((reach, reps, n, q), BF16),
            pltpu.VMEM((reach, slots, tile, tile), BF16),
            pltpu.VMEM((reach * slots + 1, tile, tile), BF16),
            pltpu.SMEM((reach * slots,), jnp.int32),
            pltpu.VMEM((n, f), F32),
            pltpu.VMEM((2, n, f), BF16),
            pltpu.VMEM((2, 2, h, f), BF16),
            pltpu.VMEM((2, 2, h, f), BF16),
            pltpu.VMEM((2, 2, q, f), BF16),
            pltpu.VMEM((2, n, f), BF16),
            pltpu.VMEM((n, f), BF16),
            pltpu.VMEM((n, f), BF16),
            pltpu.VMEM((n, f), BF16),
            pltpu.VMEM((f, n), BF16),
            pltpu.VMEM((2 * ZS, piece, f), BF16),
            pltpu.VMEM((2 * ZS, piece, f), BF16),
            pltpu.VMEM((XS, piece, f), BF16),
            pltpu.VMEM((YL * reps, piece, f), BF16),
            pltpu.VMEM((2 * ZS, piece, f), BF16),
            pltpu.VMEM((2 * ZS, piece, f), F32),
            dma((3,)),
            dma((16,)),
            dma((4, reps)),
            dma((reach, reps)),
            dma((4, 2 * reps)),
            dma((reach, 2 * reps)),
            dma((2, 6)),
            dma((2, 6)),
            dma((2, 6)),
            dma((2, 6)),
            dma((4, 2 * ZS)),
            dma((4, 2 * ZS)),
        ],
        compiler_params=pltpu.CompilerParams(
            collective_id=0, vmem_limit_bytes=56 << 20
        ),
    )(node_feats, weight, cotangent, tile_values[0], tile_coords, tile_counts)
    return (activated, input_grad, weight_grad.reshape(f, f))


def solution(mesh):
    return jax.shard_map(
        functools.partial(per_device, mesh.shape["rows"], mesh.shape["rep"]),
        mesh=mesh,
        in_specs=(
            P("rows", None),
            P(),
            P("rows", None),
            P("rows", None, "rep", None, None),
            P(None, "rows", None, "rep"),
            P("rows", None),
        ),
        out_specs=(P("rows", None), P("rows", None), P()),
        check_vma=False,
    )
```

```python
import functools

import jax
import jax.numpy as jnp
from jax import lax
from jax.experimental import pallas as pl
from jax.experimental.pallas import tpu as pltpu
from jax.sharding import PartitionSpec as P

MESH = pl.DeviceIdType.MESH
BF16 = jnp.bfloat16
F32 = jnp.float32
ZS, XS, YL = 8, 4, 2


def matmul(a, b):
    return jnp.dot(a, b, preferred_element_type=F32)


def layer_kernel(
    groups,
    reps,
    scale,
    x_hbm,
    w_ref,
    ct_hbm,
    tiles_hbm,
    coords_ref,
    counts_ref,
    act_ref,
    ig_ref,
    wg_ref,
    px,
    ad,
    dense,
    tl,
    tp,
    code,
    acc,
    send,
    ra,
    cb,
    rf,
    g,
    ctv,
    v,
    xt,
    ws,
    w1,
    w2,
    w3,
    wf,
    wp,
    load_sem,
    x_send,
    x_recv,
    a_send,
    a_recv,
    rs_send,
    rs_recv,
    ag_send,
    ag_recv,
    w_send,
    w_recv,
):
    me = lax.axis_index("rows")
    p = lax.axis_index("rep")
    up, dn = lax.rem(me + 2, groups), lax.rem(me + groups - 2, groups)
    odd = lax.rem(me, 2)
    mate = me + 1 - 2 * odd
    nxt, prv, opp = (lax.rem(p + k, reps) for k in (1, reps - 1, 2))
    n, f = acc.shape
    q = n // reps
    h = q // 2
    reach, slots, tile, _ = tl.shape
    blocks = n // tile
    out_slot = 1 + 2 * odd
    mate_slot = 3 - 2 * odd
    fwd_slot = 4 - 4 * odd
    far_slot = 4 * odd

    def rows(start, size):
        return pl.ds(pl.multiple_of(start, h), size)

    def remote(src, dst, ssem, rsem, dev):
        return pltpu.make_async_remote_copy(
            src_ref=src, dst_ref=dst, send_sem=ssem, recv_sem=rsem, device_id=dev, device_id_type=MESH
        )

    z = lax.rem(me // 2, ZS)
    x = lax.rem(me // (2 * ZS), XS)
    y_lo = me // (2 * ZS * XS)
    y = p * YL + y_lo

    def z_peer(k, core):
        other = lax.rem(z + k, ZS)
        return core * ZS + other, (me + 2 * (other - z) + core - odd, p)

    def x_peer(k):
        other = lax.rem(x + k, XS)
        return other, (me + 2 * ZS * (other - x), p)

    def y_peer(k):
        other = lax.rem(y + k, YL * reps)
        return other, (me + 2 * ZS * XS * (lax.rem(other, YL) - y_lo), other // YL)

    z_peers = [z_peer(k, core) for k in range(1, ZS) for core in range(2)]
    z_peers.append(((1 - odd) * ZS + z, (mate, p)))
    spot = odd * ZS + z
    x_peers = [x_peer(k) for k in range(1, XS)]
    y_peers = [y_peer(k) for k in range(1, YL * reps)]
    greet = [(up, p), (dn, p)] + [dev for _, dev in z_peers + x_peers + y_peers]

    barrier = pltpu.get_barrier_semaphore()
    for dev in greet:
        pl.semaphore_signal(barrier, inc=1, device_id=dev, device_id_type=MESH)

    loads = [
        pltpu.make_async_copy(src, dst, load_sem.at[i])
        for i, (src, dst) in enumerate(((tiles_hbm, tl), (x_hbm, px.at[2]), (ct_hbm, ctv)))
    ]
    for load in loads:
        load.start()

    pl.semaphore_wait(barrier, len(greet))

    def panel_copy(src, dst, ssem, rsem, kind, chunk, size):
        part = rows(chunk * size, size)
        slot = (0, 4, out_slot, mate_slot)[kind]
        dev = ((up, p), (dn, p), (mate, p), (mate, p))[kind]
        source = dst.at[fwd_slot, part] if kind == 3 else src.at[part]
        return remote(source, dst.at[slot, part], ssem.at[kind, chunk], rsem.at[slot, chunk], dev)

    def panel_wait(dst, ssem, rsem, slot, chunk, size):
        part = dst.at[slot, rows(chunk * size, size)]
        remote(part, part, ssem.at[0, chunk], rsem.at[slot, chunk], (mate, p)).wait_recv()

    def x_copy(kind, chunk):
        return panel_copy(x_hbm, px, x_send, x_recv, kind, chunk, h)

    def x_wait(slot, at):
        panel_wait(px, x_send, x_recv, slot, 2 * at, h)
        panel_wait(px, x_send, x_recv, slot, 2 * at + 1, h)

    def a_copy(kind, chunk):
        return panel_copy(ad.at[2], ad, a_send, a_recv, kind, chunk, h)

    def a_wait(slot, at):
        panel_wait(ad, a_send, a_recv, slot, 2 * at, h)
        panel_wait(ad, a_send, a_recv, slot, 2 * at + 1, h)

    def x_forward(at):
        for half in range(2):
            panel_wait(px, x_send, x_recv, fwd_slot, 2 * at + half, h)
            x_copy(3, 2 * at + half).start()

    def a_forward(chunk):
        panel_wait(ad, a_send, a_recv, fwd_slot, chunk, h)
        a_copy(3, chunk).start()

    @pl.loop(0, 2 * reps)
    def _(i):
        for kind in range(3):
            x_copy(kind, i).start()

    first = p * slots

    @pl.loop(0, reach)
    def _(d):
        for k in range(slots):
            live = first + k < counts_ref[0, d]
            at = coords_ref[0, 0, d, k] * blocks + coords_ref[1, 0, d, k]
            code[d * slots + k] = jnp.where(live, at, -1)

    tp[reach * slots] = jnp.zeros((tile, tile), BF16)
    loads[0].wait()

    @pl.loop(0, reach)
    def _(d):
        for k in range(slots):
            total = tl[d, k].astype(F32)
            for j in range(k + 1, slots):
                same = jnp.where(code[d * slots + j] == code[d * slots + k], 1.0, 0.0).astype(F32)
                total = total + same * tl[d, j].astype(F32)
            tp[d * slots + k] = total.astype(BF16)

    @pl.loop(0, reach * blocks)
    def _(t):
        d = t // blocks
        b = lax.rem(t, blocks)
        part = pl.ds(pl.multiple_of(b * tile, tile), tile)
        for c in range(blocks):
            found = jnp.int32(reach * slots)
            for k in range(slots - 1, -1, -1):
                found = jnp.where(code[d * slots + k] == b * blocks + c, d * slots + k, found)
            width = q // tile
            dense[d, c // width, part, (c % width) * tile : (c % width + 1) * tile] = tp[found]

    loads[1].wait()
    w = w_ref[...]

    sent = []

    def go(copy):
        copy.start()
        sent.append(copy)
        return copy

    def absorb(slot, chunk, panel, init=False):
        term = matmul(dense[slot, chunk], panel)
        acc[...] = term if init else acc[...] + term

    def x_panel(slot, chunk):
        return matmul(px[slot, rows(chunk * q, q), :], w).astype(BF16)

    def x_whole(slot, init=False):
        for i in range(reps):
            v[pl.ds(i * q, q), :] = x_panel(slot, i)
        total = None if init else acc[...]
        for i in range(reps):
            term = matmul(dense[slot, i], v[pl.ds(i * q, q), :])
            total = term if total is None else total + term
        acc[...] = total

    def rs_start(ph, chunk, panel):
        ssem, rsem = rs_send.at[ph], rs_recv.at[ph]
        buf = send.at[ph]

        def block(at):
            part = rows(at * q, q)
            total = acc[part, :] + matmul(dense[out_slot, chunk, part, :], panel())
            acc[part, :] = total
            buf[part, :] = total.astype(BF16)

        block(opp)
        first_hop = [
            go(remote(buf.at[rows(opp * q, h)], ra.at[ph, 0], ssem.at[0], rsem.at[0], (me, nxt))),
            go(remote(buf.at[rows(opp * q + h, h)], ra.at[ph, 1], ssem.at[1], rsem.at[1], (me, prv))),
        ]
        block(nxt)
        last_hop = [
            go(remote(buf.at[rows(nxt * q + h, h)], rf.at[ph, 0, pl.ds(h, h)], ssem.at[2], rsem.at[2], (me, nxt))),
        ]
        block(prv)
        last_hop.append(
            go(remote(buf.at[rows(prv * q, h)], rf.at[ph, 1, pl.ds(0, h)], ssem.at[3], rsem.at[3], (me, prv)))
        )
        block(p)
        return first_hop, last_hop

    x_whole(2, True)
    x_forward(0)

    @pl.loop(0, reps)
    def _(i):
        x_wait(mate_slot, i)

    x_whole(mate_slot)

    @pl.loop(0, reps)
    def _(i):
        xt[:, rows(i * q, q)] = px[2, rows(i * q, q), :].T

    @pl.loop(0, reps - 1)
    def _(i):
        absorb(fwd_slot, i, x_panel(fwd_slot, i))
        x_wait(far_slot, i)
        absorb(far_slot, i, x_panel(far_slot, i))
        x_forward(i + 1)
        x_wait(out_slot, i)
        absorb(out_slot, i, x_panel(out_slot, i))

    last = reps - 1
    x_wait(far_slot, last)

    @pl.loop(0, 2)
    def _(i):
        slot = jnp.where(i == 0, fwd_slot, far_slot)
        absorb(slot, last, x_panel(slot, last))

    x_wait(out_slot, last)
    v[pl.ds(0, q), :] = x_panel(out_slot, last)

    def rs_middle(ph, copies):
        ssem, rsem = rs_send.at[ph], rs_recv.at[ph]
        first_hop, last_hop = copies
        for k, (start, dev) in enumerate(((nxt * q, nxt), (prv * q + h, prv))):
            first_hop[k].wait_recv()
            cb[ph, k] = (ra[ph, k].astype(F32) + acc[rows(start, h), :]).astype(BF16)
            last_hop.append(
                go(remote(cb.at[ph, k], rf.at[ph, k, pl.ds(k * h, h)], ssem.at[4 + k], rsem.at[4 + k], (me, dev)))
            )
        return last_hop

    def rs_finish(ph, last_hop):
        for copy in last_hop:
            copy.wait_recv()
        return acc[rows(p * q, q), :] + rf[ph, 0].astype(F32) + rf[ph, 1].astype(F32)

    def ag_copy(ph, k, at, half, dev):
        part = g.at[ph, rows(at * q + half * h, h)]
        return remote(part, part, ag_send.at[ph, k], ag_recv.at[ph, k], (me, dev))

    def ag_start(ph):
        go(ag_copy(ph, 0, p, 0, nxt))
        go(ag_copy(ph, 1, p, 1, prv))
        go(ag_copy(ph, 2, p, 1, nxt))
        go(ag_copy(ph, 3, p, 0, prv))

    def ag_wait(ph, k):
        at, half = ((prv, 0), (nxt, 1), (prv, 1), (nxt, 0), (opp, 0), (opp, 1))[k]
        ag_copy(ph, k, at, half, prv).wait_recv()
        if k < 2:
            go(ag_copy(ph, 4 + k, at, half, (nxt, prv)[k]))

    def store_out(start, size):
        part = rows(start, size)
        ig_ref[part, :] = g[1, part, :]

    g[0, rows(p * q, q), :] = rs_finish(0, rs_middle(0, rs_start(0, last, lambda: v[pl.ds(0, q), :]))).astype(BF16)
    ag_start(0)
    loads[2].wait()

    def activate(at, half):
        start = at * q + half * h
        part = rows(start, h)
        value = g[0, part, :].astype(F32)
        sig = jax.nn.sigmoid(value)
        ad[2, part, :] = (ctv[part, :].astype(F32) * (sig * (1.0 + value * (1.0 - sig)))).astype(BF16)
        for kind in range(3):
            a_copy(kind, 2 * at + half).start()
        act_ref[part, :] = (value * sig).astype(BF16)

    def a_panel(slot, chunk):
        return ad[slot, rows(chunk * q, q), :]

    activate(p, 0)
    activate(p, 1)
    absorb(2, p, a_panel(2, p), True)
    ag_wait(0, 0)
    activate(prv, 0)
    ag_wait(0, 1)
    activate(nxt, 1)
    a_forward(2 * p)
    a_forward(2 * p + 1)
    ag_wait(0, 2)
    activate(prv, 1)
    ag_wait(0, 3)
    activate(nxt, 0)
    a_wait(mate_slot, p)
    absorb(mate_slot, p, a_panel(mate_slot, p))
    absorb(fwd_slot, p, a_panel(fwd_slot, p))
    ag_wait(0, 4)
    activate(opp, 0)
    ag_wait(0, 5)
    activate(opp, 1)
    a_forward(2 * prv)
    a_forward(2 * nxt + 1)
    a_wait(far_slot, p)
    a_wait(out_slot, p)

    @pl.loop(0, 2)
    def _(i):
        slot = jnp.where(i == 0, far_slot, out_slot)
        absorb(slot, p, a_panel(slot, p))

    a_forward(2 * prv + 1)
    a_forward(2 * nxt)
    for at in (prv, nxt, opp):
        a_wait(mate_slot, at)

    @pl.loop(0, 6)
    def _(i):
        at = jnp.where(i // 2 == 0, prv, jnp.where(i // 2 == 1, nxt, opp))
        slot = jnp.where(lax.rem(i, 2) == 0, 2, mate_slot)
        absorb(slot, at, a_panel(slot, at))

    for at in (prv, nxt):
        a_wait(far_slot, at)
        a_wait(out_slot, at)

    @pl.loop(0, 6)
    def _(i):
        at = jnp.where(i < 3, prv, nxt)
        turn = lax.rem(i, 3)
        slot = jnp.where(turn == 0, fwd_slot, jnp.where(turn == 1, far_slot, out_slot))
        absorb(slot, at, a_panel(slot, at))

    a_forward(2 * opp)
    a_forward(2 * opp + 1)
    a_wait(far_slot, opp)

    @pl.loop(0, 2)
    def _(i):
        slot = jnp.where(i == 0, fwd_slot, far_slot)
        absorb(slot, opp, a_panel(slot, opp))

    a_wait(out_slot, opp)

    def w_go(step, to, src, dst, slot, dev):
        go(remote(src, dst, w_send.at[step, to], w_recv.at[step, slot], dev))

    def w_wait(step, ref, slot):
        remote(ref, ref, w_send.at[step, 0], w_recv.at[step, slot], (mate, p)).wait_recv()

    copies = rs_start(1, opp, lambda: a_panel(out_slot, opp))
    piece = f // (2 * ZS)
    wp[...] = (matmul(xt[...], send[1]) * scale).reshape(2 * ZS, piece, f)
    ws[...] = wp[...].astype(BF16)
    for other, dev in z_peers:
        w_go(0, other, ws.at[other], w1.at[spot], spot, dev)
    last_hop = rs_middle(1, copies)
    part = wp[spot]
    for other, dev in z_peers:
        w_wait(0, w1.at[other], other)
        part = part + w1[other].astype(F32)
    w2[x] = part.astype(BF16)
    for other, dev in x_peers:
        w_go(1, other, w2.at[x], w2.at[x], x, dev)
    for other, dev in x_peers:
        w_wait(1, w2.at[other], other)
    w3[y] = sum(w2[k].astype(F32) for k in range(XS)).astype(BF16)
    for other, dev in y_peers:
        w_go(2, other, w3.at[y], w3.at[y], y, dev)
    back = rs_finish(1, last_hop).astype(BF16)
    g[1, rows(p * q, q), :] = lax.dot_general(
        back, w, (((1,), (1,)), ((), ())), preferred_element_type=F32
    ).astype(BF16)
    ag_start(1)
    store_out(p * q, q)
    ag_wait(1, 0)
    ag_wait(1, 1)
    for other, dev in y_peers:
        w_wait(2, w3.at[other], other)
    wf[spot] = sum(w3[k].astype(F32) for k in range(YL * reps)).astype(BF16)
    for other, dev in z_peers:
        w_go(3, other, wf.at[spot], wf.at[spot], spot, dev)
    ag_wait(1, 2)
    store_out(prv * q, q)
    ag_wait(1, 3)
    store_out(nxt * q, q)
    for other, dev in z_peers:
        w_wait(3, wf.at[other], other)
    wg_ref[...] = wf[...].astype(F32)
    ag_wait(1, 4)
    ag_wait(1, 5)
    store_out(opp * q, q)

    for copy in sent:
        copy.wait_send()

    @pl.loop(0, 2 * reps)
    def _(i):
        for kind in range(4):
            x_copy(kind, i).wait_send()
            a_copy(kind, i).wait_send()


def per_device(groups, reps, node_feats, weight, cotangent, tile_values, tile_coords, tile_counts):
    n, f = node_feats.shape
    _, reach, slots, tile, _ = tile_values.shape
    q = n // reps
    h = q // 2
    dma = pltpu.SemaphoreType.DMA
    piece = f // (2 * ZS)
    hbm = pl.BlockSpec(memory_space=pl.ANY)
    vmem = pl.BlockSpec(memory_space=pltpu.VMEM)
    smem = pl.BlockSpec(memory_space=pltpu.SMEM)
    activated, input_grad, weight_grad = pl.pallas_call(
        functools.partial(layer_kernel, groups, reps, (n * groups) ** (-0.5)),
        out_shape=(
            pltpu.VMEM((n, f), BF16),
            pltpu.VMEM((n, f), BF16),
            pltpu.VMEM((2 * ZS, piece, f), F32),
        ),
        in_specs=[hbm, vmem, hbm, hbm, smem, smem],
        out_specs=(vmem, vmem, vmem),
        scratch_shapes=[
            pltpu.VMEM((reach, n, f), BF16),
            pltpu.VMEM((reach, n, f), BF16),
            pltpu.VMEM((reach, reps, n, q), BF16),
            pltpu.VMEM((reach, slots, tile, tile), BF16),
            pltpu.VMEM((reach * slots + 1, tile, tile), BF16),
            pltpu.SMEM((reach * slots,), jnp.int32),
            pltpu.VMEM((n, f), F32),
            pltpu.VMEM((2, n, f), BF16),
            pltpu.VMEM((2, 2, h, f), BF16),
            pltpu.VMEM((2, 2, h, f), BF16),
            pltpu.VMEM((2, 2, q, f), BF16),
            pltpu.VMEM((2, n, f), BF16),
            pltpu.VMEM((n, f), BF16),
            pltpu.VMEM((n, f), BF16),
            pltpu.VMEM((f, n), BF16),
            pltpu.VMEM((2 * ZS, piece, f), BF16),
            pltpu.VMEM((2 * ZS, piece, f), BF16),
            pltpu.VMEM((XS, piece, f), BF16),
            pltpu.VMEM((YL * reps, piece, f), BF16),
            pltpu.VMEM((2 * ZS, piece, f), BF16),
            pltpu.VMEM((2 * ZS, piece, f), F32),
            dma((3,)),
            dma((4, 2 * reps)),
            dma((reach, 2 * reps)),
            dma((4, 2 * reps)),
            dma((reach, 2 * reps)),
            dma((2, 6)),
            dma((2, 6)),
            dma((2, 6)),
            dma((2, 6)),
            dma((4, 2 * ZS)),
            dma((4, 2 * ZS)),
        ],
        compiler_params=pltpu.CompilerParams(
            collective_id=0, vmem_limit_bytes=56 << 20
        ),
    )(node_feats, weight, cotangent, tile_values[0], tile_coords, tile_counts)
    return (activated, input_grad, weight_grad.reshape(f, f))


def solution(mesh):
    return jax.shard_map(
        functools.partial(per_device, mesh.shape["rows"], mesh.shape["rep"]),
        mesh=mesh,
        in_specs=(
            P("rows", None),
            P(),
            P("rows", None),
            P("rows", None, "rep", None, None),
            P(None, "rows", None, "rep"),
            P("rows", None),
        ),
        out_specs=(P("rows", None), P("rows", None), P()),
        check_vma=False,
    )
```
